32 devices in a mesh: groups: 2 (over y), zone: 4 (over x, core), tile: 4 (over z).
Axes of the slice: x: 2, y: 2, z: 4, core: 2. Of those that a mesh axis runs over, the one named last changes fastest.
Arguments:
- backscatter: bfloat16 [8, 2, 256, 512], P(('groups', 'zone'), None, 'tile'), parts along dimension 0, may hold values from -6 to 6
- row_bank: bfloat16 [16, 128, 128], replicated, may hold values from -0.3125 to 0.3125
- row_index: int32 [8, 4, 3], P(('groups', 'zone')), parts along dimension 0, may hold values from 0 to 3
- row_pick: int32 [8, 4, 3], P(('groups', 'zone')), parts along dimension 0, may hold values from 0 to 15
- row_mask: int32 [8, 4, 3], P(('groups', 'zone')), parts along dimension 0, may hold values 0 or 1
- column_bank: bfloat16 [16, 128, 128], replicated, may hold values from -0.3125 to 0.3125
- column_index: int32 [8, 2, 3], P(('groups', 'zone')), parts along dimension 0, may hold values from 0 to 1
- column_pick: int32 [8, 2, 3], P(('groups', 'zone')), parts along dimension 0, may hold values from 0 to 15
- column_mask: int32 [8, 2, 3], P(('groups', 'zone')), parts along dimension 0, may hold values 0 or 1
Outputs:
- geocoded: bfloat16 [8, 2, 256, 512], P(('groups', 'zone'), None, None, 'tile'), parts along dimension 0
The draws below stay inside these ranges and needn't reach their ends.
There are 2 independent parts, one for each index of `groups`. The reference program is written for one: setup_inputs(seed, part) draws one part's arguments, and reference() takes and returns one part's arrays. A program takes and returns all parts, laid end to end along the dimension named above; an argument that names none is the same for every part. Nothing has to cross between parts.
All inputs are finite; a program needn't handle non-finite values. No bound on the sum of `row_mask` or of `column_mask` on one device may be relied on, other than what follows from the above.
Results may differ from the reference program's by a relative error of at most 0.0049.
Values may be sent and summed in bfloat16 or wider, within the bound.
No kernel may reach another device: no remote copies, remote signals or barrier semaphores. Data moves between devices by JAX's collectives and lax.ppermute only.
A program may use at most 64 MiB of HBM per device.

```python
import jax
import jax.numpy as jnp
from jax import lax

BLOCK = 128
EDGE = 64
NBANK = 16
ZONES = 4
LINES = 256
ROWS = 256
SAMPLES = 512
COLUMN_BLOCKS = 4
LINE_BLOCKS = 2


def place_ends(drawn, rng, low, largest):
    spot = [jax.random.randint(jax.random.fold_in(rng, axis), (), 0, length) for axis, length in enumerate(drawn.shape)]
    longest = drawn.shape.index(max(drawn.shape))
    neighbour = spot[:longest] + [(spot[longest] + 1) % drawn.shape[longest]] + spot[longest + 1:]
    return drawn.at[tuple(spot)].set(low).at[tuple(neighbour)].set(largest)


def steps_of(own_key, dims, shards, least, high):
    factor_of = 1.0
    for position, parts in shards:
        heights = jax.random.uniform(jax.random.fold_in(jax.random.fold_in(own_key, 6), position), (parts,), jnp.float32, least / len(shards), high / len(shards))
        factor_of = factor_of * jnp.repeat(jnp.exp(heights), dims[position] // parts).reshape((-1,) + (1,) * (len(dims) - 1 - position))
    return factor_of


def normal_values(own_key, dims, width, bound, cuts=(), held_as=jnp.bfloat16):
    entries = jax.random.normal(own_key, dims, jnp.float32) * width
    if len(cuts) > 0:
        entries = steps_of(own_key, dims, cuts, -0.22, 0.18) * entries
    return jnp.clip(entries, min=-bound, max=bound).astype(held_as)


def setup_inputs(seed: int = 0, part: int = 0) -> dict:
    arg_keys = jax.random.split(jax.random.key(seed), 10)
    part_keys = jax.random.split(jax.random.fold_in(arg_keys[9], part), 10)
    return {
        "backscatter": normal_values(part_keys[0], (ZONES, 2, LINES, SAMPLES), 1.0, 6.0, ((0, 4), (2, 4))),
        "row_bank": normal_values(arg_keys[1], (NBANK, BLOCK, BLOCK), (3 * BLOCK) ** -0.5, 0.3125),
        "row_index": place_ends(jax.random.randint(part_keys[2], (ZONES, COLUMN_BLOCKS, 3), 0, COLUMN_BLOCKS), jax.random.fold_in(part_keys[2], 1), 0, COLUMN_BLOCKS - 1).astype(jnp.int32),
        "row_pick": place_ends(jax.random.randint(part_keys[3], (ZONES, COLUMN_BLOCKS, 3), 0, NBANK), jax.random.fold_in(part_keys[3], 1), 0, NBANK - 1).astype(jnp.int32),
        "row_mask": place_ends((jax.random.randint(part_keys[4], (ZONES, COLUMN_BLOCKS, 3), 0, 4) < 3).astype(jnp.int32), jax.random.fold_in(part_keys[4], 1), 0, 1),
        "column_bank": normal_values(arg_keys[5], (NBANK, BLOCK, BLOCK), (3 * BLOCK) ** -0.5, 0.3125),
        "column_index": place_ends(jax.random.randint(part_keys[6], (ZONES, LINE_BLOCKS, 3), 0, LINE_BLOCKS), jax.random.fold_in(part_keys[6], 1), 0, LINE_BLOCKS - 1).astype(jnp.int32),
        "column_pick": place_ends(jax.random.randint(part_keys[7], (ZONES, LINE_BLOCKS, 3), 0, NBANK), jax.random.fold_in(part_keys[7], 1), 0, NBANK - 1).astype(jnp.int32),
        "column_mask": place_ends((jax.random.randint(part_keys[8], (ZONES, LINE_BLOCKS, 3), 0, 4) < 3).astype(jnp.int32), jax.random.fold_in(part_keys[8], 1), 0, 1),
    }


def resample_rows(image, index, pick, mask, row_bank):
    blocks = image.reshape(2, LINES, COLUMN_BLOCKS, BLOCK)

    def per_block(item):
        band_index, band_pick, band_mask = item
        gathered = blocks[:, :, band_index, :].astype(jnp.float32)
        weights = row_bank[band_pick].astype(jnp.float32) * band_mask.astype(jnp.float32)[:, None, None]
        return jnp.einsum("clbi,bij->clj", gathered, weights).astype(jnp.bfloat16)

    stacked = lax.map(per_block, (index, pick, mask))
    return jnp.transpose(stacked, (1, 2, 0, 3)).reshape(2, LINES, SAMPLES)


def resample_columns(image, index, pick, mask, column_bank):
    blocks = image.reshape(2, LINE_BLOCKS, BLOCK, SAMPLES)

    def per_block(item):
        band_index, band_pick, band_mask = item
        gathered = blocks[:, band_index].astype(jnp.float32)
        weights = column_bank[band_pick].astype(jnp.float32) * band_mask.astype(jnp.float32)[:, None, None]
        return jnp.einsum("cbik,boi->cok", gathered, weights).astype(jnp.bfloat16)

    stacked = lax.map(per_block, (index, pick, mask))
    return jnp.transpose(stacked, (1, 0, 2, 3)).reshape(2, ROWS, SAMPLES)


def reference(backscatter, row_bank, row_index, row_pick, row_mask, column_bank, column_index, column_pick, column_mask):
    def per_zone(entry):
        image, rindex, rpick, rmask, cindex, cpick, cmask = entry
        along_samples = resample_rows(image, rindex, rpick, rmask, row_bank)
        return resample_columns(along_samples, cindex, cpick, cmask, column_bank)

    gridded = lax.map(per_zone, (backscatter, row_index, row_pick, row_mask, column_index, column_pick, column_mask))
    feather = ((jnp.arange(EDGE, dtype=jnp.float32) + 0.5) / EDGE)[:, None]
    bottoms = gridded[:-1, :, ROWS - EDGE:, :].astype(jnp.float32)
    tops = gridded[1:, :, :EDGE, :].astype(jnp.float32)
    blended = ((1.0 - feather) * bottoms + feather * tops).astype(jnp.bfloat16)
    gridded = gridded.at[:-1, :, ROWS - EDGE:, :].set(blended)
    gridded = gridded.at[1:, :, :EDGE, :].set(blended)
    return gridded
```

```python
import jax
import jax.numpy as jnp
from jax import lax
from jax.experimental import pallas as pl
from jax.experimental.pallas import tpu as pltpu
from jax.sharding import PartitionSpec as P

BLOCK = 128
EDGE = 64
VMEM = pl.BlockSpec(memory_space=pltpu.VMEM)
SMEM = pl.BlockSpec(memory_space=pltpu.SMEM)
ANY = pl.BlockSpec(memory_space=pl.ANY)
HBM = pl.BlockSpec(memory_space=pltpu.HBM)


def each(count, body):
    if count <= 4:
        for i in range(count):
            body(i)
    else:
        pl.loop(0, count)(body)


def shape(*dims, dtype=jnp.bfloat16):
    return jax.ShapeDtypeStruct(dims, dtype)


def params(*arrays):
    held = sum(a.size * a.dtype.itemsize for a in arrays)
    return dict(
        compiler_params=pltpu.CompilerParams(vmem_limit_bytes=2 * held + (1 << 20)),
        cost_estimate=pl.CostEstimate(flops=10**8, bytes_accessed=held, transcendentals=0),
    )


def rows_kernel(index, pick, mask, image_hbm, bank_hbm, *refs):
    *outs, index_s, pick_s, mask_s, image, bank, sems = refs
    pairs = ((index, index_s), (pick, pick_s), (mask, mask_s), (image_hbm, image), (bank_hbm, bank))
    copies = [pltpu.make_async_copy(a, b, sems.at[k]) for k, (a, b) in enumerate(pairs)]
    for copy in copies:
        copy.start()
    for copy in copies:
        copy.wait()
    channels, lines, _ = image.shape[1:]
    tile = lax.axis_index("tile")

    def write(q, out):
        total = jnp.zeros((channels * lines, BLOCK), jnp.float32)
        for b in range(index.shape[0]):
            start = pl.multiple_of(index_s[b, 0, q] * BLOCK, BLOCK)
            source = image[0, :, :, pl.ds(start, BLOCK)].reshape(channels * lines, BLOCK)
            term = jnp.dot(source, bank[pick_s[b, 0, q]], preferred_element_type=jnp.float32)
            total += term * mask_s[b, 0, q].astype(jnp.float32)
        out[...] = total.astype(jnp.bfloat16).reshape(channels, lines, BLOCK)

    if len(outs) > 1:
        for d, out in enumerate(outs):
            write(jnp.bitwise_xor(tile, d), out)
    else:
        each(outs[0].shape[0], lambda q: write(q, outs[0].at[q]))


def weights_kernel(index, pick, mask, bank, high, low, mine, other):
    blocks = high.shape[0]
    for r in range(blocks):
        for s in range(blocks):
            total = jnp.zeros((BLOCK, BLOCK), jnp.float32)
            for b in range(index.shape[2]):
                used = jnp.where(index[0, r, b] == s, mask[0, r, b], 0).astype(jnp.float32)
                total += bank[pick[0, r, b]].astype(jnp.float32) * used
            rounded = total.astype(jnp.bfloat16)
            columns = slice(s * BLOCK, (s + 1) * BLOCK)
            high[r, :, columns] = rounded
            low[r, :, columns] = (total - rounded.astype(jnp.float32)).astype(jnp.bfloat16)
    coefficients(mine, other)


def coefficients(mine, other):
    zone = lax.axis_index("zone")
    row = lax.broadcasted_iota(jnp.int32, (EDGE, BLOCK), 0).astype(jnp.float32)
    feather = (row + 0.5) / EDGE
    lower = zone < lax.axis_size("zone") - 1
    upper = zone > 0
    mine[0] = jnp.where(upper, feather, 1.0)
    other[0] = jnp.where(upper, 1.0 - feather, 0.0)
    mine[1] = jnp.where(lower, 1.0 - feather, 1.0)
    other[1] = jnp.where(lower, feather, 0.0)


def columns_kernel(high, low, *refs):
    *lines, grid, first, second, held = refs
    tile = lax.axis_index("tile")
    channels, depth, _ = lines[0].shape
    for d, ref in enumerate(lines):
        start = pl.multiple_of(jnp.bitwise_xor(tile, d) * depth, depth)
        for c in range(channels):
            held[pl.ds(start, depth), c * BLOCK : (c + 1) * BLOCK] = ref[c]
    source = held[...]
    for r in range(high.shape[0]):
        total = jnp.dot(high[r], source, preferred_element_type=jnp.float32)
        total += jnp.dot(low[r], source, preferred_element_type=jnp.float32)
        for c in range(channels):
            part = total[:, c * BLOCK : (c + 1) * BLOCK].astype(jnp.bfloat16)
            grid[c, r * BLOCK : (r + 1) * BLOCK] = part
    pick_edges(grid, first, second)


def edge_starts(rows):
    even = lax.axis_index("zone") % 2 == 0
    last = rows - EDGE
    return (
        pl.multiple_of(jnp.where(even, last, 0), EDGE),
        pl.multiple_of(jnp.where(even, 0, last), EDGE),
    )


def pick_edges(grid, first, second):
    one, two = edge_starts(grid.shape[1])
    first[...] = grid[:, pl.ds(one, EDGE)]
    second[...] = grid[:, pl.ds(two, EDGE)]


def general_columns_kernel(index, pick, mask, bank, lines, grid, first, second, mine, other):
    tiles, channels, depth, _ = lines.shape
    span = BLOCK // depth

    def block(r):
        for c in range(channels):
            total = jnp.zeros((BLOCK, BLOCK), jnp.float32)
            for b in range(index.shape[2]):
                source = lines[pl.ds(index[0, r, b] * span, span), c].reshape(BLOCK, BLOCK)
                term = jnp.dot(bank[pick[0, r, b]], source, preferred_element_type=jnp.float32)
                total += term * mask[0, r, b].astype(jnp.float32)
            start = pl.multiple_of(r * BLOCK, BLOCK)
            grid[c, pl.ds(start, BLOCK)] = total.astype(jnp.bfloat16)

    each(index.shape[1], block)
    pick_edges(grid, first, second)
    coefficients(mine, other)


def blend_kernel(mine, other, grid, first, second, out, edges, sems):
    rows = grid.shape[1]
    middle = pltpu.make_async_copy(
        grid.at[:, EDGE : rows - EDGE], out.at[0, :, EDGE : rows - EDGE], sems.at[0]
    )
    middle.start()
    copies = [middle]
    even = lax.axis_index("zone") % 2 == 0
    sides = (jnp.where(even, 1, 0), jnp.where(even, 0, 1))
    for k, (came, side, start) in enumerate(zip((first, second), sides, edge_starts(rows))):
        own = grid[:, pl.ds(start, EDGE)].astype(jnp.float32)
        edges[k] = (mine[side] * own + other[side] * came[...].astype(jnp.float32)).astype(jnp.bfloat16)
        copy = pltpu.make_async_copy(edges.at[k], out.at[0, :, pl.ds(start, EDGE)], sems.at[1 + k])
        copy.start()
        copies.append(copy)
    for copy in copies:
        copy.wait()


def on_device(image, row_bank, row_index, row_pick, row_mask, column_bank, column_index, column_pick, column_mask):
    channels, depth, samples = image.shape[1:]
    blocks = row_index.shape[1]
    line_blocks = column_index.shape[1]
    rows = line_blocks * BLOCK
    tiles = lax.axis_size("tile")
    zones = lax.axis_size("zone")
    small = tiles == 4 and blocks == tiles and line_blocks * BLOCK <= 256
    turned = lambda table: jnp.transpose(table, (2, 0, 1))
    panel = shape(channels, depth, BLOCK)
    sent = [panel] * tiles if small else [shape(blocks, channels, depth, BLOCK)]
    along = pl.pallas_call(
        rows_kernel,
        out_shape=sent,
        in_specs=[HBM] * 5,
        out_specs=[VMEM] * len(sent),
        scratch_shapes=[pltpu.SMEM(turned(row_index).shape, jnp.int32)] * 3
        + [pltpu.VMEM(image.shape, image.dtype), pltpu.VMEM(row_bank.shape, row_bank.dtype)]
        + [pltpu.SemaphoreType.DMA((5,))],
        **params(image, row_bank, *sent),
    )(*(pltpu.with_memory_space_constraint(v, pltpu.HBM) for v in (turned(row_index), turned(row_pick), turned(row_mask), image, row_bank)))
    edge = shape(channels, EDGE, BLOCK)
    grid = shape(channels, rows, BLOCK)
    sides = shape(2, EDGE, BLOCK, dtype=jnp.float32)
    if small:
        dense = shape(line_blocks, BLOCK, rows)
        high, low, mine, other = pl.pallas_call(
            weights_kernel,
            out_shape=(dense, dense, sides, sides),
            in_specs=[SMEM] * 3 + [VMEM],
            out_specs=(VMEM,) * 4,
            **params(column_bank, dense, dense, sides, sides),
        )(column_index, column_pick, column_mask, column_bank)
        lines = [along[0]]
        for d in range(1, tiles):
            lines.append(lax.ppermute(along[d], "tile", [(i, i ^ d) for i in range(tiles)]))
        grid, first, second = pl.pallas_call(
            columns_kernel,
            out_shape=(grid, edge, edge),
            in_specs=[VMEM] * (2 + tiles),
            out_specs=(VMEM,) * 3,
            scratch_shapes=[pltpu.VMEM((rows, channels * BLOCK), jnp.bfloat16)],
            **params(dense, dense, *lines, grid),
        )(high, low, *lines)
    else:
        lines = lax.all_to_all(along[0], "tile", split_axis=0, concat_axis=0, tiled=True)
        grid, first, second, mine, other = pl.pallas_call(
            general_columns_kernel,
            out_shape=(grid, edge, edge, sides, sides),
            in_specs=[SMEM] * 3 + [VMEM] * 2,
            out_specs=(VMEM,) * 5,
            **params(column_bank, lines, grid, edge, edge, sides, sides),
        )(column_index, column_pick, column_mask, column_bank, lines)
    second = lax.ppermute(second, "zone", [(z, ((z + 1) ^ 1) - 1 if 0 < ((z + 1) ^ 1) <= zones else zones - 1 - z) for z in range(zones)])
    first = lax.ppermute(first, "zone", [(z, z ^ 1) for z in range(zones)])
    return pl.pallas_call(
        blend_kernel,
        out_shape=shape(1, channels, rows, BLOCK),
        in_specs=[VMEM] * 5,
        out_specs=ANY,
        scratch_shapes=[pltpu.VMEM((2, channels, EDGE, BLOCK), jnp.bfloat16), pltpu.SemaphoreType.DMA((3,))],
        **params(mine, other, grid, first, second),
    )(mine, other, grid, first, second)


def solution(mesh):
    zoned = P(("groups", "zone"), None, None)
    in_specs = (P(("groups", "zone"), None, "tile", None), P(), zoned, zoned, zoned, P(), zoned, zoned, zoned)
    out_specs = P(("groups", "zone"), None, None, "tile")
    return jax.shard_map(on_device, mesh=mesh, in_specs=in_specs, out_specs=out_specs, check_vma=False)
```

```python
import jax
import jax.numpy as jnp
from jax import lax
from jax.experimental import pallas as pl
from jax.experimental.pallas import tpu as pltpu
from jax.sharding import PartitionSpec as P


BLOCK = 128
EDGE = 64
ROUTES = ((0, 1, 2, 3), (2, 3, 1, 0), (3, 2, 0, 1), (1, 0, 3, 2))
VMEM = pl.BlockSpec(memory_space=pltpu.VMEM)
SMEM = pl.BlockSpec(memory_space=pltpu.SMEM)
ANY = pl.BlockSpec(memory_space=pl.ANY)
HBM = pl.BlockSpec(memory_space=pltpu.HBM)


def each(count, body):
    if count <= 4:
        for i in range(count):
            body(i)
    else:
        pl.loop(0, count)(body)


def shape(*dims, dtype=jnp.bfloat16):
    return jax.ShapeDtypeStruct(dims, dtype)


def params(*arrays):
    held = sum(a.size * a.dtype.itemsize for a in arrays)
    return dict(
        compiler_params=pltpu.CompilerParams(vmem_limit_bytes=2 * held + (1 << 20)),
        cost_estimate=pl.CostEstimate(flops=10**8, bytes_accessed=held, transcendentals=0),
    )


def looked_up(table, place):
    return sum(jnp.where(place == i, entry, 0) for i, entry in enumerate(table))


def rows_kernel(index, pick, mask, image_hbm, bank_hbm, *refs):
    *outs, index_s, pick_s, mask_s, image, bank, sems = refs
    pairs = ((index, index_s), (pick, pick_s), (mask, mask_s), (image_hbm, image), (bank_hbm, bank))
    copies = [pltpu.make_async_copy(a, b, sems.at[k]) for k, (a, b) in enumerate(pairs)]
    for copy in copies:
        copy.start()
    for copy in copies:
        copy.wait()
    channels, lines, _ = image.shape[1:]
    tile = lax.axis_index("tile")

    def write(q, out):
        total = jnp.zeros((channels * lines, BLOCK), jnp.float32)
        for b in range(index.shape[0]):
            start = pl.multiple_of(index_s[b, 0, q] * BLOCK, BLOCK)
            source = image[0, :, :, pl.ds(start, BLOCK)].reshape(channels * lines, BLOCK)
            term = jnp.dot(source, bank[pick_s[b, 0, q]], preferred_element_type=jnp.float32)
            total += term * mask_s[b, 0, q].astype(jnp.float32)
        out[...] = total.astype(jnp.bfloat16).reshape(channels, lines, BLOCK)

    if len(outs) > 1:
        for d, out in enumerate(outs):
            write(looked_up(ROUTES[d], tile), out)
    else:
        each(outs[0].shape[0], lambda q: write(q, outs[0].at[q]))


def weights_kernel(index, pick, mask, bank, high, low, mine, other):
    blocks = high.shape[0]
    for r in range(blocks):
        for s in range(blocks):
            total = jnp.zeros((BLOCK, BLOCK), jnp.float32)
            for b in range(index.shape[2]):
                used = jnp.where(index[0, r, b] == s, mask[0, r, b], 0).astype(jnp.float32)
                total += bank[pick[0, r, b]].astype(jnp.float32) * used
            rounded = total.astype(jnp.bfloat16)
            columns = slice(s * BLOCK, (s + 1) * BLOCK)
            high[r, :, columns] = rounded
            low[r, :, columns] = (total - rounded.astype(jnp.float32)).astype(jnp.bfloat16)
    coefficients(mine, other)


def coefficients(mine, other):
    zone = lax.axis_index("zone")
    row = lax.broadcasted_iota(jnp.int32, (EDGE, BLOCK), 0).astype(jnp.float32)
    feather = (row + 0.5) / EDGE
    lower = zone < lax.axis_size("zone") - 1
    upper = zone > 0
    mine[0] = jnp.where(upper, feather, 1.0)
    other[0] = jnp.where(upper, 1.0 - feather, 0.0)
    mine[1] = jnp.where(lower, 1.0 - feather, 1.0)
    other[1] = jnp.where(lower, feather, 0.0)


def columns_kernel(high, low, *refs):
    *lines, grid, first, second, held = refs
    tile = lax.axis_index("tile")
    channels, depth, _ = lines[0].shape
    for d, ref in enumerate(lines):
        came_from = [ROUTES[d].index(i) for i in range(len(lines))]
        start = pl.multiple_of(looked_up(came_from, tile) * depth, depth)
        for c in range(channels):
            held[pl.ds(start, depth), c * BLOCK : (c + 1) * BLOCK] = ref[c]
    source = held[...]
    for r in range(high.shape[0]):
        total = jnp.dot(high[r], source, preferred_element_type=jnp.float32)
        total += jnp.dot(low[r], source, preferred_element_type=jnp.float32)
        for c in range(channels):
            part = total[:, c * BLOCK : (c + 1) * BLOCK].astype(jnp.bfloat16)
            grid[c, r * BLOCK : (r + 1) * BLOCK] = part
    pick_edges(grid, first, second)


def edge_starts(rows):
    even = lax.axis_index("zone") % 2 == 0
    last = rows - EDGE
    return (
        pl.multiple_of(jnp.where(even, last, 0), EDGE),
        pl.multiple_of(jnp.where(even, 0, last), EDGE),
    )


def pick_edges(grid, first, second):
    one, two = edge_starts(grid.shape[1])
    first[...] = grid[:, pl.ds(one, EDGE)]
    second[...] = grid[:, pl.ds(two, EDGE)]


def general_columns_kernel(index, pick, mask, bank, lines, grid, first, second, mine, other):
    _, channels, depth, _ = lines.shape
    span = BLOCK // depth

    def block(r):
        for c in range(channels):
            total = jnp.zeros((BLOCK, BLOCK), jnp.float32)
            for b in range(index.shape[2]):
                source = lines[pl.ds(index[0, r, b] * span, span), c].reshape(BLOCK, BLOCK)
                term = jnp.dot(bank[pick[0, r, b]], source, preferred_element_type=jnp.float32)
                total += term * mask[0, r, b].astype(jnp.float32)
            start = pl.multiple_of(r * BLOCK, BLOCK)
            grid[c, pl.ds(start, BLOCK)] = total.astype(jnp.bfloat16)

    each(index.shape[1], block)
    pick_edges(grid, first, second)
    coefficients(mine, other)


def blend_kernel(mine, other, grid, first, second, out, edges, sems):
    rows = grid.shape[1]
    middle = pltpu.make_async_copy(
        grid.at[:, EDGE : rows - EDGE], out.at[0, :, EDGE : rows - EDGE], sems.at[0]
    )
    middle.start()
    copies = [middle]
    even = lax.axis_index("zone") % 2 == 0
    sides = (jnp.where(even, 1, 0), jnp.where(even, 0, 1))
    for k, (came, side, start) in enumerate(zip((first, second), sides, edge_starts(rows))):
        own = grid[:, pl.ds(start, EDGE)].astype(jnp.float32)
        edges[k] = (mine[side] * own + other[side] * came[...].astype(jnp.float32)).astype(jnp.bfloat16)
        copy = pltpu.make_async_copy(edges.at[k], out.at[0, :, pl.ds(start, EDGE)], sems.at[1 + k])
        copy.start()
        copies.append(copy)
    for copy in copies:
        copy.wait()


def on_device(image, row_bank, row_index, row_pick, row_mask, column_bank, column_index, column_pick, column_mask):
    channels, depth, _ = image.shape[1:]
    blocks = row_index.shape[1]
    line_blocks = column_index.shape[1]
    rows = line_blocks * BLOCK
    tiles = lax.axis_size("tile")
    zones = lax.axis_size("zone")
    small = tiles == 4 and blocks == tiles and line_blocks * BLOCK <= 256
    turned = lambda table: jnp.transpose(table, (2, 0, 1))
    panel = shape(channels, depth, BLOCK)
    sent = [panel] * tiles if small else [shape(blocks, channels, depth, BLOCK)]
    along = pl.pallas_call(
        rows_kernel,
        out_shape=sent,
        in_specs=[HBM] * 5,
        out_specs=[VMEM] * len(sent),
        scratch_shapes=[pltpu.SMEM(turned(row_index).shape, jnp.int32)] * 3
        + [pltpu.VMEM(image.shape, image.dtype), pltpu.VMEM(row_bank.shape, row_bank.dtype)]
        + [pltpu.SemaphoreType.DMA((5,))],
        **params(image, row_bank, *sent),
    )(*(pltpu.with_memory_space_constraint(v, pltpu.HBM) for v in (turned(row_index), turned(row_pick), turned(row_mask), image, row_bank)))
    edge = shape(channels, EDGE, BLOCK)
    grid = shape(channels, rows, BLOCK)
    sides = shape(2, EDGE, BLOCK, dtype=jnp.float32)
    if small:
        dense = shape(line_blocks, BLOCK, rows)
        high, low, mine, other = pl.pallas_call(
            weights_kernel,
            out_shape=(dense, dense, sides, sides),
            in_specs=[SMEM] * 3 + [VMEM],
            out_specs=(VMEM,) * 4,
            **params(column_bank, dense, dense, sides, sides),
        )(column_index, column_pick, column_mask, column_bank)
        lines = [along[0]]
        for d in range(1, tiles):
            lines.append(lax.ppermute(along[d], "tile", list(enumerate(ROUTES[d]))))
        grid, first, second = pl.pallas_call(
            columns_kernel,
            out_shape=(grid, edge, edge),
            in_specs=[VMEM] * (2 + tiles),
            out_specs=(VMEM,) * 3,
            scratch_shapes=[pltpu.VMEM((rows, channels * BLOCK), jnp.bfloat16)],
            **params(dense, dense, *lines, grid),
        )(high, low, *lines)
    else:
        lines = lax.all_to_all(along[0], "tile", split_axis=0, concat_axis=0, tiled=True)
        grid, first, second, mine, other = pl.pallas_call(
            general_columns_kernel,
            out_shape=(grid, edge, edge, sides, sides),
            in_specs=[SMEM] * 3 + [VMEM] * 2,
            out_specs=(VMEM,) * 5,
            **params(column_bank, lines, grid, edge, edge, sides, sides),
        )(column_index, column_pick, column_mask, column_bank, lines)
    second = lax.ppermute(second, "zone", [(z, ((z + 1) ^ 1) - 1 if 0 < ((z + 1) ^ 1) <= zones else zones - 1 - z) for z in range(zones)])
    first = lax.ppermute(first, "zone", [(z, z ^ 1) for z in range(zones)])
    return pl.pallas_call(
        blend_kernel,
        out_shape=shape(1, channels, rows, BLOCK),
        in_specs=[VMEM] * 5,
        out_specs=ANY,
        scratch_shapes=[pltpu.VMEM((2, channels, EDGE, BLOCK), jnp.bfloat16), pltpu.SemaphoreType.DMA((3,))],
        **params(mine, other, grid, first, second),
    )(mine, other, grid, first, second)


def solution(mesh):
    zoned = P(("groups", "zone"), None, None)
    in_specs = (P(("groups", "zone"), None, "tile", None), P(), zoned, zoned, zoned, P(), zoned, zoned, zoned)
    out_specs = P(("groups", "zone"), None, None, "tile")
    return jax.shard_map(on_device, mesh=mesh, in_specs=in_specs, out_specs=out_specs, check_vma=False)
```

```python
import jax
import jax.numpy as jnp
from jax import lax
from jax.experimental import pallas as pl
from jax.experimental.pallas import tpu as pltpu
from jax.sharding import PartitionSpec as P


BLOCK = 128
EDGE = 64
SPLIT = 1
ROUTES = ((0, 1, 2, 3), (2, 3, 1, 0), (3, 2, 0, 1), (1, 0, 3, 2))
VMEM = pl.BlockSpec(memory_space=pltpu.VMEM)
SMEM = pl.BlockSpec(memory_space=pltpu.SMEM)
ANY = pl.BlockSpec(memory_space=pl.ANY)
HBM = pl.BlockSpec(memory_space=pltpu.HBM)


def each(count, body):
    if count <= 4:
        for i in range(count):
            body(i)
    else:
        pl.loop(0, count)(body)


def shape(*dims, dtype=jnp.bfloat16):
    return jax.ShapeDtypeStruct(dims, dtype)


def params(*arrays):
    held = sum(a.size * a.dtype.itemsize for a in arrays)
    return dict(
        compiler_params=pltpu.CompilerParams(vmem_limit_bytes=2 * held + (1 << 20)),
        cost_estimate=pl.CostEstimate(flops=10**8, bytes_accessed=held, transcendentals=0),
    )


def looked_up(table, place):
    return sum(jnp.where(place == i, entry, 0) for i, entry in enumerate(table))


def rows_kernel(index, pick, mask, image_hbm, bank_hbm, *refs):
    *outs, index_s, pick_s, mask_s, image, bank, sems = refs
    pairs = [(index, index_s), (pick, pick_s), (mask, mask_s)]
    for k in range(SPLIT):
        part = pl.ds(k * bank.shape[0] // SPLIT, bank.shape[0] // SPLIT)
        pairs.append((bank_hbm.at[part], bank.at[part]))
    pairs.append((image_hbm, image))
    copies = [pltpu.make_async_copy(a, b, sems.at[k]) for k, (a, b) in enumerate(pairs)]
    for copy in copies:
        copy.start()
    for copy in copies:
        copy.wait()
    channels, lines, _ = image.shape[1:]
    tile = lax.axis_index("tile")

    def write(q, out):
        sources, kernels = [], []
        for b in range(index.shape[0]):
            start = pl.multiple_of(index_s[b, 0, q] * BLOCK, BLOCK)
            source = image[0, :, :, pl.ds(start, BLOCK)].reshape(channels * lines, BLOCK)
            sources.append(source * mask_s[b, 0, q].astype(jnp.float32).astype(jnp.bfloat16))
            kernels.append(bank[pick_s[b, 0, q]])
        total = jnp.dot(
            jnp.concatenate(sources, axis=1),
            jnp.concatenate(kernels, axis=0),
            preferred_element_type=jnp.float32,
        )
        out[...] = total.astype(jnp.bfloat16).reshape(channels, lines, BLOCK)

    if len(outs) > 1:
        for d, out in enumerate(outs):
            write(looked_up(ROUTES[d], tile), out)
    else:
        each(outs[0].shape[0], lambda q: write(q, outs[0].at[q]))


def weights_kernel(index, pick, mask, bank, high, low, mine, other):
    blocks = high.shape[0]
    for r in range(blocks):
        for s in range(blocks):
            total = jnp.zeros((BLOCK, BLOCK), jnp.float32)
            for b in range(index.shape[2]):
                used = jnp.where(index[0, r, b] == s, mask[0, r, b], 0).astype(jnp.float32)
                total += bank[pick[0, r, b]].astype(jnp.float32) * used
            rounded = total.astype(jnp.bfloat16)
            columns = slice(s * BLOCK, (s + 1) * BLOCK)
            high[r, :, columns] = rounded
            low[r, :, columns] = (total - rounded.astype(jnp.float32)).astype(jnp.bfloat16)
    coefficients(mine, other)


def coefficients(mine, other):
    zone = lax.axis_index("zone")
    row = lax.broadcasted_iota(jnp.int32, (EDGE, BLOCK), 0).astype(jnp.float32)
    feather = (row + 0.5) / EDGE
    lower = zone < lax.axis_size("zone") - 1
    upper = zone > 0
    mine[0] = jnp.where(upper, feather, 1.0)
    other[0] = jnp.where(upper, 1.0 - feather, 0.0)
    mine[1] = jnp.where(lower, 1.0 - feather, 1.0)
    other[1] = jnp.where(lower, feather, 0.0)


def columns_kernel(high, low, *refs):
    *lines, grid, top, bottom, near, held = refs
    tile = lax.axis_index("tile")
    channels, depth, _ = lines[0].shape
    for d, ref in enumerate(lines):
        came_from = [ROUTES[d].index(i) for i in range(len(lines))]
        start = pl.multiple_of(looked_up(came_from, tile) * depth, depth)
        for c in range(channels):
            held[pl.ds(start, depth), c * BLOCK : (c + 1) * BLOCK] = ref[c]
    source = held[...]
    for r in range(high.shape[0]):
        total = jnp.dot(high[r], source, preferred_element_type=jnp.float32)
        total += jnp.dot(low[r], source, preferred_element_type=jnp.float32)
        for c in range(channels):
            part = total[:, c * BLOCK : (c + 1) * BLOCK].astype(jnp.bfloat16)
            grid[c, r * BLOCK : (r + 1) * BLOCK] = part
    pick_edges(grid, top, bottom, near)


def pick_edges(grid, top, bottom, near):
    last = grid.shape[1] - EDGE
    top[...] = grid[:, :EDGE]
    bottom[...] = grid[:, last:]
    start = jnp.where(lax.axis_index("zone") % 2 == 0, last, 0)
    near[...] = grid[:, pl.ds(pl.multiple_of(start, EDGE), EDGE)]


def general_columns_kernel(index, pick, mask, bank, lines, grid, top, bottom, near, mine, other):
    _, channels, depth, _ = lines.shape
    span = BLOCK // depth

    def block(r):
        for c in range(channels):
            total = jnp.zeros((BLOCK, BLOCK), jnp.float32)
            for b in range(index.shape[2]):
                source = lines[pl.ds(index[0, r, b] * span, span), c].reshape(BLOCK, BLOCK)
                term = jnp.dot(bank[pick[0, r, b]], source, preferred_element_type=jnp.float32)
                total += term * mask[0, r, b].astype(jnp.float32)
            start = pl.multiple_of(r * BLOCK, BLOCK)
            grid[c, pl.ds(start, BLOCK)] = total.astype(jnp.bfloat16)

    each(index.shape[1], block)
    pick_edges(grid, top, bottom, near)
    coefficients(mine, other)


def from_near():
    zone = lax.axis_index("zone")
    return (zone % 2 == 1) | (lax.axis_size("zone") % 2 == 1)


def blend_kernel(mine, other, grid, below, above, out, edges, sems):
    rows = grid.shape[1]
    middle = pltpu.make_async_copy(
        grid.at[:, EDGE : rows - EDGE], out.at[0, :, EDGE : rows - EDGE], sems.at[0]
    )
    middle.start()
    copies = [middle]
    for k, (came, start) in enumerate(((above, 0), (below, rows - EDGE))):
        own = grid[:, start : start + EDGE].astype(jnp.float32)
        mixed = mine[k] * own + other[k] * came[...].astype(jnp.float32)
        if k == 0:
            mixed = jnp.where(from_near(), mixed, own)
        edges[k] = mixed.astype(jnp.bfloat16)
        copy = pltpu.make_async_copy(edges.at[k], out.at[0, :, start : start + EDGE], sems.at[1 + k])
        copy.start()
        copies.append(copy)
    for copy in copies:
        copy.wait()


def late_kernel(mine, other, grid, above, partial, out, edge, sem):
    zone = lax.axis_index("zone")

    @pl.when((zone > 0) & ~from_near())
    def _():
        own = grid[:, :EDGE].astype(jnp.float32)
        edge[...] = (mine[0] * own + other[0] * above[...].astype(jnp.float32)).astype(jnp.bfloat16)
        copy = pltpu.make_async_copy(edge, out.at[0, :, :EDGE], sem)
        copy.start()
        copy.wait()


def on_device(image, row_bank, row_index, row_pick, row_mask, column_bank, column_index, column_pick, column_mask):
    channels, depth, _ = image.shape[1:]
    blocks = row_index.shape[1]
    line_blocks = column_index.shape[1]
    rows = line_blocks * BLOCK
    tiles = lax.axis_size("tile")
    zones = lax.axis_size("zone")
    small = tiles == 4 and blocks == tiles and line_blocks * BLOCK <= 256
    turned = lambda table: jnp.transpose(table, (2, 0, 1))
    panel = shape(channels, depth, BLOCK)
    sent = [panel] * tiles if small else [shape(blocks, channels, depth, BLOCK)]
    along = pl.pallas_call(
        rows_kernel,
        out_shape=sent,
        in_specs=[HBM] * 5,
        out_specs=[VMEM] * len(sent),
        scratch_shapes=[pltpu.SMEM(turned(row_index).shape, jnp.int32)] * 3
        + [pltpu.VMEM(image.shape, image.dtype), pltpu.VMEM(row_bank.shape, row_bank.dtype)]
        + [pltpu.SemaphoreType.DMA((4 + SPLIT,))],
        **params(image, row_bank, *sent),
    )(*(pltpu.with_memory_space_constraint(v, pltpu.HBM) for v in (turned(row_index), turned(row_pick), turned(row_mask), image, row_bank)))
    edge = shape(channels, EDGE, BLOCK)
    grid = shape(channels, rows, BLOCK)
    sides = shape(2, EDGE, BLOCK, dtype=jnp.float32)
    if small:
        dense = shape(line_blocks, BLOCK, rows)
        high, low, mine, other = pl.pallas_call(
            weights_kernel,
            out_shape=(dense, dense, sides, sides),
            in_specs=[SMEM] * 3 + [VMEM],
            out_specs=(VMEM,) * 4,
            **params(column_bank, dense, dense, sides, sides),
        )(column_index, column_pick, column_mask, column_bank)
        lines = [along[0]]
        for d in range(1, tiles):
            lines.append(lax.ppermute(along[d], "tile", list(enumerate(ROUTES[d]))))
        grid, top, bottom, near = pl.pallas_call(
            columns_kernel,
            out_shape=(grid, edge, edge, edge),
            in_specs=[VMEM] * (2 + tiles),
            out_specs=(VMEM,) * 4,
            scratch_shapes=[pltpu.VMEM((rows, channels * BLOCK), jnp.bfloat16)],
            **params(dense, dense, *lines, grid),
        )(high, low, *lines)
    else:
        lines = lax.all_to_all(along[0], "tile", split_axis=0, concat_axis=0, tiled=True)
        grid, top, bottom, near, mine, other = pl.pallas_call(
            general_columns_kernel,
            out_shape=(grid, edge, edge, edge, sides, sides),
            in_specs=[SMEM] * 3 + [VMEM] * 2,
            out_specs=(VMEM,) * 6,
            **params(column_bank, lines, grid, edge, edge, sides, sides),
        )(column_index, column_pick, column_mask, column_bank, lines)
    below = lax.ppermute(top, "zone", [(z, (z - 1) % zones) for z in range(zones)])
    above = lax.ppermute(bottom, "zone", [(z, (z + 1) % zones) for z in range(zones)])
    beside = above
    if zones % 2 == 0:
        beside = lax.ppermute(near, "zone", [(z, z ^ 1) for z in range(zones)])
    out = pl.pallas_call(
        blend_kernel,
        out_shape=shape(1, channels, rows, BLOCK),
        in_specs=[VMEM] * 5,
        out_specs=ANY,
        scratch_shapes=[pltpu.VMEM((2, channels, EDGE, BLOCK), jnp.bfloat16), pltpu.SemaphoreType.DMA((3,))],
        **params(mine, other, grid, below, beside),
    )(mine, other, grid, below, beside)
    return pl.pallas_call(
        late_kernel,
        out_shape=shape(1, channels, rows, BLOCK),
        in_specs=[VMEM] * 4 + [ANY],
        out_specs=ANY,
        input_output_aliases={4: 0},
        scratch_shapes=[pltpu.VMEM((channels, EDGE, BLOCK), jnp.bfloat16), pltpu.SemaphoreType.DMA],
        **params(mine, other, grid, above),
    )(mine, other, grid, above, out)


def solution(mesh):
    zoned = P(("groups", "zone"), None, None)
    in_specs = (P(("groups", "zone"), None, "tile", None), P(), zoned, zoned, zoned, P(), zoned, zoned, zoned)
    out_specs = P(("groups", "zone"), None, None, "tile")
    return jax.shard_map(on_device, mesh=mesh, in_specs=in_specs, out_specs=out_specs, check_vma=False)
```
